32 devices in a mesh: tok: 4 (over y, core), feat: 8 (over z, x).
Axes of the slice: x: 2, y: 2, z: 4, core: 2. Of those that a mesh axis runs over, the one named last changes fastest.
Arguments:
- tokens: bfloat16 [4096, 2048], P('tok', 'feat'), may hold values from -6 to 6
- level_bits: int32 [2, 4], replicated, may hold values from 0 to 3, each once within a row
- up_blocks: bfloat16 [2, 16, 5, 128, 512], P(None, 'feat', None, None, 'tok'), may hold values from -0.21875 to 0.21875
- down_blocks: bfloat16 [2, 16, 5, 512, 128], P(None, 'feat', None, None, 'tok'), may hold values from -0.109375 to 0.109375
- rank_in: bfloat16 [2, 2048, 256], replicated, may hold values from -0.125 to 0.125
- rank_up: bfloat16 [2, 256, 8192], P(None, None, 'feat'), may hold values from -0.15625 to 0.15625
- rank_down: bfloat16 [2, 8192, 256], P(None, 'feat'), may hold values from -0.0625 to 0.0625
- rank_out: bfloat16 [2, 256, 2048], P(None, None, 'feat'), may hold values from -0.15625 to 0.15625
Outputs:
- outputs: bfloat16 [4096, 2048], P('tok', 'feat')
The draws below stay inside these ranges and needn't reach their ends.
Inputs may be any that keep to these rules, and one draw needn't show every extreme that they name: `level_bits`: each row is a permutation of the bits 0 to 3.
All inputs are finite; a program needn't handle non-finite values.
Results may differ from the reference program's by a relative error of at most 0.015.
Values may be sent and summed in bfloat16 or wider, within the bound.
A program may use at most 64 MiB of HBM per device.

```python
import jax
import jax.numpy as jnp
from jax import lax

D = 2048
HID = 8192
NB = 16
LEVELS = 4
RANK = 256
LAYERS = 2
TOK_DEV = 1024
TOKENS = 4096


def levels(rng, shape, cuts, smallest, largest):
    level = 1.0
    for dim, shards_of in cuts:
        heights = jax.random.uniform(jax.random.fold_in(jax.random.fold_in(rng, 6), dim), (shards_of,), jnp.float32, smallest / len(cuts), largest / len(cuts))
        level = level * jnp.repeat(jnp.exp(heights), shape[dim] // shards_of).reshape((-1,) + (1,) * (len(shape) - 1 - dim))
    return level


def centred(key, dims, scale, most, pieces=(), kind=jnp.bfloat16):
    drawn = jax.random.normal(key, dims, jnp.float32) * scale
    if len(pieces) > 0:
        drawn = levels(key, dims, pieces, -0.22, 0.18) * drawn
    return jnp.clip(drawn, min=-most, max=most).astype(kind)


def setup_inputs(seed: int = 0) -> dict:
    seeds = jax.random.split(jax.random.key(seed), 9)
    tokens = centred(seeds[0], (TOKENS, D), 1.0, 6.0, ((0, 4), (1, 8)))
    level_bits = jax.vmap(lambda own: jax.random.permutation(own, LEVELS))(jax.random.split(seeds[1], LAYERS)).reshape((LAYERS, LEVELS)).astype(jnp.int32)
    up_blocks = centred(seeds[2], (LAYERS, NB, LEVELS + 1, D // NB, HID // NB), ((LEVELS + 2) * (D // NB)) ** -0.5, 0.21875, ((1, 8), (4, 4)))
    down_blocks = centred(seeds[3], (LAYERS, NB, LEVELS + 1, HID // NB, D // NB), ((LEVELS + 2) * (HID // NB)) ** -0.5, 0.109375, ((1, 8), (4, 4)))
    rank_in = centred(seeds[4], (LAYERS, D, RANK), D ** -0.5, 0.125)
    rank_up = centred(seeds[5], (LAYERS, RANK, HID), ((LEVELS + 2) * RANK) ** -0.5, 0.15625, ((2, 8),))
    rank_down = centred(seeds[6], (LAYERS, HID, RANK), HID ** -0.5, 0.0625, ((1, 8),))
    rank_out = centred(seeds[7], (LAYERS, RANK, D), ((LEVELS + 2) * RANK) ** -0.5, 0.15625, ((2, 8),))
    return {"tokens": tokens, "level_bits": level_bits, "up_blocks": up_blocks, "down_blocks": down_blocks, "rank_in": rank_in, "rank_up": rank_up, "rank_down": rank_down, "rank_out": rank_out}


def block_einsum(left, right):
    return jnp.einsum("tjd,jdh->tjh", left.astype(jnp.float32), right.astype(jnp.float32))


def reference(tokens, level_bits, up_blocks, down_blocks, rank_in, rank_up, rank_down, rank_out):
    width_block = D // NB
    hidden_block = HID // NB
    block_ids = jnp.arange(NB, dtype=jnp.int32)
    current = tokens
    for layer_num in range(LAYERS):
        up_layer = up_blocks[layer_num]
        down_layer = down_blocks[layer_num]
        partners = [jnp.bitwise_xor(block_ids, jnp.left_shift(jnp.int32(1), level_bits[layer_num, level_num]).astype(jnp.int32)).astype(jnp.int32) for level_num in range(LEVELS)]

        def tile_layer(tile_rows, up_layer=up_layer, down_layer=down_layer, partners=partners, layer_num=layer_num):
            blocked = tile_rows.reshape(-1, NB, width_block)
            pre_act = block_einsum(blocked, up_layer[:, 0])
            for level_num in range(LEVELS):
                partner = jnp.take(blocked, partners[level_num], axis=1)
                pre_act = pre_act + block_einsum(partner, up_layer[:, 1 + level_num])
            latent = jnp.dot(tile_rows, rank_in[layer_num], preferred_element_type=jnp.float32).astype(jnp.bfloat16)
            pre_act = pre_act + jnp.dot(latent, rank_up[layer_num], preferred_element_type=jnp.float32).reshape(-1, NB, hidden_block)
            hidden = jax.nn.gelu(pre_act, approximate=False).astype(jnp.bfloat16)
            result = block_einsum(hidden, down_layer[:, 0])
            for level_num in range(LEVELS):
                moved = jnp.take(hidden, partners[level_num], axis=1)
                moved_weight = jnp.take(down_layer[:, 1 + level_num], partners[level_num], axis=0)
                result = result + block_einsum(moved, moved_weight)
            latent_back = jnp.dot(hidden.reshape(-1, HID), rank_down[layer_num], preferred_element_type=jnp.float32).astype(jnp.bfloat16)
            result = result + jnp.dot(latent_back, rank_out[layer_num], preferred_element_type=jnp.float32).reshape(-1, NB, width_block)
            return (tile_rows.astype(jnp.float32) + result.reshape(-1, D)).astype(jnp.bfloat16)

        tiles = current.reshape(TOKENS // TOK_DEV, TOK_DEV, D)
        current = lax.map(tile_layer, tiles).reshape(TOKENS, D)
    return current
```

```python
import functools
import math

import jax
import jax.numpy as jnp
from jax import lax
from jax.experimental import pallas as pl
from jax.experimental.pallas import tpu as pltpu
from jax.sharding import PartitionSpec as P

CHUNK_ROWS = 256
SKEW = 2
MESH = pl.DeviceIdType.MESH


def bits_of(count):
    return count.bit_length() - 1


def network(cfg, tokens, level_bits, up_in, down_in, rank_in, rank_up, rank_down, rank_out, out, *scratch):
    (xbuf, xrecv, tsend, trecv, part, half, full, hid, acc, wup, wdown) = scratch[:11]
    rest = scratch[11:]
    layers, rows, width = cfg["layers"], cfg["rows"], cfg["width"]
    blocks, wb, hb = cfg["blocks"], cfg["wb"], cfg["hb"]
    n_feat, n_tok, rank = cfg["n_feat"], cfg["n_tok"], cfg["rank"]
    cr = cfg["chunk"]
    chunks = rows // cr
    local_bits = bits_of(blocks)
    nb = bits_of(n_feat)
    levels = local_bits + nb
    gather = cfg["gather"]
    if gather:
        upg, downg = rest[:layers], rest[layers : 2 * layers]
        wsend, wrecv, wloc = rest[2 * layers : 2 * layers + 3]
        rest = rest[2 * layers + 3 :]
    else:
        upg = [up_in.at[l] for l in range(layers)]
        downg = [down_in.at[l] for l in range(layers)]
    xs_sem, xr_sem, ts_sem, tr_sem, as_sem, ar_sem = rest

    me = lax.axis_index("feat")
    me_tok = lax.axis_index("tok")
    mybit = [(me // (1 << b)) % 2 for b in range(nb)]
    partner = [me + (1 << b) * (1 - 2 * mybit[b]) for b in range(nb)]

    barrier = pltpu.get_barrier_semaphore()
    for b in range(nb):
        pl.semaphore_signal(barrier, inc=1, device_id={"feat": partner[b]}, device_id_type=MESH)
    greeted = nb
    if gather:
        for o in range(1, n_tok):
            pl.semaphore_signal(
                barrier, inc=1, device_id={"tok": lax.rem(me_tok + o, n_tok)}, device_id_type=MESH
            )
        greeted += n_tok - 1
    pl.semaphore_wait(barrier, greeted)

    def weight_copy(l, kind, o):
        if kind == 0:
            cols = up_in.shape[-1]
            src = up_in.at[l]
            dst = upg[l].at[:, :, :, pl.ds(pl.multiple_of(me_tok * cols, cols), cols)]
        else:
            cols = down_in.shape[-2]
            src = down_in.at[l]
            dst = downg[l].at[:, :, pl.ds(pl.multiple_of(me_tok * cols, cols), cols), :]
        if o == 0:
            return pltpu.make_async_copy(src, dst, wloc.at[l, kind])
        return pltpu.make_async_remote_copy(
            src_ref=src,
            dst_ref=dst,
            send_sem=wsend.at[l, kind, o - 1],
            recv_sem=wrecv.at[l, kind, o - 1],
            device_id={"tok": lax.rem(me_tok + o, n_tok)},
            device_id_type=MESH,
        )

    def start_weights():
        for l in range(layers):
            for kind in range(2):
                for o in range(n_tok):
                    weight_copy(l, kind, o).start()

    prepared = set()

    def prepare(l, kind):
        if (l, kind) in prepared:
            return
        prepared.add((l, kind))
        if gather:
            for o in range(n_tok):
                copy = weight_copy(l, kind, o)
                copy.wait() if o == 0 else copy.wait_recv()
        order = []
        for b in range(levels):
            at = 0
            for k in range(levels):
                at = jnp.maximum(at, jnp.where(level_bits[l, k] == b, 1 + k, 0))
            order.append(at)
        for j in range(blocks):
            if kind == 0:
                wup[l, j, pl.ds(0, wb), :] = upg[l][j, 0]
                for b in range(levels):
                    wup[l, j, pl.ds((1 + b) * wb, wb), :] = upg[l][j, order[b]]
                wup[l, j, pl.ds((1 + levels) * wb, rank), :] = rank_up[l, :, pl.ds(j * hb, hb)]
            else:
                wdown[l, j, pl.ds(0, wb), :] = downg[l][j, 0]
                for b in range(levels):
                    wdown[l, j, pl.ds((1 + b) * wb, wb), :] = downg[l][j, order[b]]

    def x_copy(l, c, b):
        at = pl.ds(c * cr, cr)
        return pltpu.make_async_remote_copy(
            src_ref=xbuf.at[l, at, :],
            dst_ref=xrecv.at[l, b, at, :],
            send_sem=xs_sem.at[l, c, b],
            recv_sem=xr_sem.at[l, c, b],
            device_id={"feat": partner[b]},
            device_id_type=MESH,
        )

    def t_copy(l, c, b):
        at = pl.ds(c * cr, cr)
        return pltpu.make_async_remote_copy(
            src_ref=tsend.at[l, b, at, :],
            dst_ref=trecv.at[l, b, at, :],
            send_sem=ts_sem.at[l, c, b],
            recv_sem=tr_sem.at[l, c, b],
            device_id={"feat": partner[b]},
            device_id_type=MESH,
        )

    last = nb - 1
    sizes = [cr >> (k + 1) for k in range(last)]
    own_at = [0]
    for k in range(last):
        own_at.append(own_at[-1] + mybit[k] * sizes[k])
    away_at = [own_at[k] + (1 - mybit[k]) * sizes[k] for k in range(last)]
    piece = cr >> last
    half_at = [sum(sizes[:k]) for k in range(last + 1)]
    half_rows = half_at[-1] + piece

    def reduce_copy(u, c, k):
        if k < last:
            src = part.at[u, pl.ds(pl.multiple_of(c * cr + away_at[k], sizes[k]), sizes[k]), :]
            size = sizes[k]
        else:
            src = part.at[u, pl.ds(pl.multiple_of(c * cr + own_at[last], piece), piece), :]
            size = piece
        return pltpu.make_async_remote_copy(
            src_ref=src,
            dst_ref=half.at[u, pl.ds(c * half_rows + half_at[k], size), :],
            send_sem=as_sem.at[u, c, k],
            recv_sem=ar_sem.at[u, c, k],
            device_id={"feat": partner[k]},
            device_id_type=MESH,
        )

    def spread_copy(u, c, k):
        size = cr >> (k + 1)
        at = pl.ds(pl.multiple_of(c * cr + own_at[k + 1], size), size)
        return pltpu.make_async_remote_copy(
            src_ref=full.at[u, at, :],
            dst_ref=full.at[u, at, :],
            send_sem=as_sem.at[u, c, nb + k],
            recv_sem=ar_sem.at[u, c, nb + k],
            device_id={"feat": partner[k]},
            device_id_type=MESH,
        )

    def sum_stage(u, c, k):
        reduce_copy(u, c, k).wait_recv()
        size = sizes[k] if k < last else piece
        start = own_at[k + 1] if k < last else own_at[last]
        at = pl.ds(pl.multiple_of(c * cr + start, size), size)
        total = part[u, at, :].astype(jnp.float32) + half[
            u, pl.ds(c * half_rows + half_at[k], size), :
        ].astype(jnp.float32)
        if k < last:
            part[u, at, :] = total.astype(jnp.bfloat16)
            reduce_copy(u, c, k + 1).start()
        else:
            full[u, at, :] = total.astype(jnp.bfloat16)
            if last > 0:
                spread_copy(u, c, last - 1).start()

    def spread_stage(u, c, k):
        spread_copy(u, c, k).wait_recv()
        if k > 0:
            spread_copy(u, c, k - 1).start()

    def sum_stages(u, c):
        found = [functools.partial(sum_stage, u, c, k) for k in range(nb)]
        for k in range(last - 1, 0, -1):
            found.append(functools.partial(spread_stage, u, c, k))
        return found

    def finish_sum(u, c):
        if last > 0:
            spread_stage(u, c, 0)

    def begin(l, c):
        at = pl.ds(c * cr, cr)
        u = 2 * l
        x = xbuf[l, at, :]
        mine = rank_in[l, pl.ds(pl.multiple_of(me * width, width), width), :]
        part[u, at, :] = jnp.dot(x, mine, preferred_element_type=jnp.float32).astype(jnp.bfloat16)
        reduce_copy(u, c, 0).start()
        for b in reversed(range(nb)):
            x_copy(l, c, b).start()

    def first(c):
        at = pl.ds(c * cr, cr)
        xbuf[0, at, :] = tokens[at, :]
        begin(0, c)

    def middle(l, c):
        at = pl.ds(c * cr, cr)
        u = 2 * l + 1
        prepare(l, 0)
        finish_sum(u - 1, c)
        for b in range(nb):
            x_copy(l, c, b).wait_recv()
        for j in range(blocks):
            pieces = [xbuf[l, at, pl.ds(j * wb, wb)]]
            for b in range(local_bits):
                pieces.append(xbuf[l, at, pl.ds((j ^ (1 << b)) * wb, wb)])
            for b in range(nb):
                pieces.append(xrecv[l, b, at, pl.ds(j * wb, wb)])
            pieces.append(full[u - 1, at, :])
            pre = jnp.dot(
                jnp.concatenate(pieces, axis=1), wup[l, j], preferred_element_type=jnp.float32
            )
            act = 0.5 * pre * (1.0 + lax.erf(pre * (1.0 / math.sqrt(2.0))))
            hid[at, pl.ds(j * hb, hb)] = act.astype(jnp.bfloat16)
        part[u, at, :] = jnp.dot(
            hid[at, :], rank_down[l], preferred_element_type=jnp.float32
        ).astype(jnp.bfloat16)
        reduce_copy(u, c, 0).start()
        prepare(l, 1)
        own = [None] * blocks
        for j in range(blocks):
            out_j = lax.dot_general(
                hid[at, pl.ds(j * hb, hb)],
                wdown[l, j],
                (((1,), (1,)), ((), ())),
                preferred_element_type=jnp.float32,
            )
            terms = [out_j[:, k * wb : (k + 1) * wb] for k in range(1 + levels)]
            for b in range(nb):
                tsend[l, b, at, pl.ds(j * wb, wb)] = terms[1 + local_bits + b].astype(jnp.bfloat16)
            for to, value in [(j, terms[0])] + [(j ^ (1 << b), terms[1 + b]) for b in range(local_bits)]:
                own[to] = value if own[to] is None else own[to] + value
        for b in reversed(range(nb)):
            t_copy(l, c, b).start()
        for j in range(blocks):
            col = pl.ds(j * wb, wb)
            acc[at, col] = own[j] + xbuf[l, at, col].astype(jnp.float32)

    def close(l, c):
        at = pl.ds(c * cr, cr)
        u = 2 * l + 1
        finish_sum(u, c)
        total = acc[at, :] + jnp.dot(full[u, at, :], rank_out[l], preferred_element_type=jnp.float32)
        for b in range(nb):
            t_copy(l, c, b).wait_recv()
            total = total + trecv[l, b, at, :].astype(jnp.float32)
        result = total.astype(jnp.bfloat16)
        if l + 1 < layers:
            xbuf[l + 1, at, :] = result
            begin(l + 1, c)
        else:
            out[at, :] = result

    plan = []
    for c in range(chunks):
        steps = [functools.partial(first, c)]
        for l in range(layers):
            steps += sum_stages(2 * l, c)
            steps.append(functools.partial(middle, l, c))
            steps += sum_stages(2 * l + 1, c)
            steps.append(functools.partial(close, l, c))
        plan.append(steps)

    plan[0][0]()
    if gather:
        start_weights()
    for tick in range(1, len(plan[0]) + cfg["skew"] * (chunks - 1)):
        for c in range(chunks):
            at = tick - cfg["skew"] * c
            if 0 <= at < len(plan[c]):
                plan[c][at]()

    for l in range(layers):
        if gather:
            for kind in range(2):
                for o in range(1, n_tok):
                    weight_copy(l, kind, o).wait_send()
        for c in range(chunks):
            for b in range(nb):
                x_copy(l, c, b).wait_send()
                t_copy(l, c, b).wait_send()
            for u in (2 * l, 2 * l + 1):
                for k in range(nb):
                    reduce_copy(u, c, k).wait_send()
                for k in range(last):
                    spread_copy(u, c, k).wait_send()


def per_device(tokens, level_bits, up_blocks, down_blocks, rank_in, rank_up, rank_down, rank_out):
    rows, width = tokens.shape
    layers, blocks, parts, wb, up_cols = up_blocks.shape
    hb, down_cols = down_blocks.shape[3:]
    n_tok, n_feat = lax.axis_size("tok"), lax.axis_size("feat")
    rank = rank_in.shape[-1]
    hidden = blocks * hb
    nb = bits_of(n_feat)
    chunk = min(CHUNK_ROWS, rows)
    chunks = rows // chunk
    gather = n_tok > 1 and up_cols % 128 == 0 and down_cols % 16 == 0
    if not gather:
        up_blocks = lax.all_gather(up_blocks, "tok", axis=4, tiled=True)
        down_blocks = lax.all_gather(down_blocks, "tok", axis=4, tiled=True)
    down_blocks = jnp.swapaxes(down_blocks, 3, 4)
    cfg = dict(
        layers=layers, rows=rows, width=width, blocks=blocks, wb=wb, hb=hb, n_feat=n_feat,
        n_tok=n_tok, rank=rank, chunk=chunk, gather=gather, skew=SKEW,
    )
    bf16 = jnp.bfloat16
    uses = 2 * layers
    half_rows = chunk
    scratch = [
        pltpu.VMEM((layers, rows, width), bf16),
        pltpu.VMEM((layers, nb, rows, width), bf16),
        pltpu.VMEM((layers, nb, rows, width), bf16),
        pltpu.VMEM((layers, nb, rows, width), bf16),
        pltpu.VMEM((uses, rows, rank), bf16),
        pltpu.VMEM((uses, chunks * half_rows, rank), bf16),
        pltpu.VMEM((uses, rows, rank), bf16),
        pltpu.VMEM((rows, hidden), bf16),
        pltpu.VMEM((rows, width), jnp.float32),
        pltpu.VMEM((layers, blocks, parts * wb + rank, hb), bf16),
        pltpu.VMEM((layers, blocks, parts * wb, hb), bf16),
    ]
    dma = pltpu.SemaphoreType.DMA
    if gather:
        scratch += [pltpu.VMEM((blocks, parts, wb, hb), bf16)] * (2 * layers)
        scratch += [
            dma((layers, 2, n_tok - 1)),
            dma((layers, 2, n_tok - 1)),
            dma((layers, 2)),
        ]
    scratch += [dma((layers, chunks, nb))] * 4 + [dma((uses, chunks, 2 * nb - 1))] * 2
    vmem = pl.BlockSpec(memory_space=pltpu.VMEM)
    smem = pl.BlockSpec(memory_space=pltpu.SMEM)
    return pl.pallas_call(
        functools.partial(network, cfg),
        out_shape=jax.ShapeDtypeStruct((rows, width), bf16),
        in_specs=[vmem, smem] + [vmem] * 6,
        out_specs=vmem,
        scratch_shapes=scratch,
        compiler_params=pltpu.CompilerParams(
            collective_id=0, has_side_effects=True, vmem_limit_bytes=63 * 1024 * 1024
        ),
    )(tokens, level_bits, up_blocks, down_blocks, rank_in, rank_up, rank_down, rank_out)


def solution(mesh):
    return jax.shard_map(
        per_device,
        mesh=mesh,
        in_specs=(
            P("tok", "feat"),
            P(),
            P(None, "feat", None, None, "tok"),
            P(None, "feat", None, None, "tok"),
            P(),
            P(None, None, "feat"),
            P(None, "feat", None),
            P(None, None, "feat"),
        ),
        out_specs=P("tok", "feat"),
        check_vma=False,
    )
```

```python
import functools
import math

import jax
import jax.numpy as jnp
from jax import lax
from jax.experimental import pallas as pl
from jax.experimental.pallas import tpu as pltpu
from jax.sharding import PartitionSpec as P

CHUNK_ROWS = 256
SKEW = 1
LATER = 1
MESH = pl.DeviceIdType.MESH


def bits_of(count):
    return count.bit_length() - 1


def network(cfg, tokens, level_bits, up_in, down_in, rank_in, rank_up, rank_down, rank_out, out, *scratch):
    (xbuf, xrecv, tsend, trecv, part, half, full, hid, acc, wup, wdown) = scratch[:11]
    rest = scratch[11:]
    layers, rows, width = cfg["layers"], cfg["rows"], cfg["width"]
    blocks, wb, hb = cfg["blocks"], cfg["wb"], cfg["hb"]
    n_feat, n_tok, rank = cfg["n_feat"], cfg["n_tok"], cfg["rank"]
    cr = cfg["chunk"]
    chunks = rows // cr
    local_bits = bits_of(blocks)
    nb = bits_of(n_feat)
    levels = local_bits + nb
    gather = cfg["gather"]
    if gather:
        upg, downg = rest[:layers], rest[layers : 2 * layers]
        wsend, wrecv, wloc = rest[2 * layers : 2 * layers + 3]
        rest = rest[2 * layers + 3 :]
    else:
        upg = [up_in.at[l] for l in range(layers)]
        downg = [down_in.at[l] for l in range(layers)]
    xs_sem, xr_sem, ts_sem, tr_sem, as_sem, ar_sem = rest

    me = lax.axis_index("feat")
    me_tok = lax.axis_index("tok")
    mybit = [(me // (1 << b)) % 2 for b in range(nb)]
    partner = [me + (1 << b) * (1 - 2 * mybit[b]) for b in range(nb)]

    barrier = pltpu.get_barrier_semaphore()
    for b in range(nb):
        pl.semaphore_signal(barrier, inc=1, device_id={"feat": partner[b]}, device_id_type=MESH)
    greeted = nb
    if gather:
        for o in range(1, n_tok):
            pl.semaphore_signal(
                barrier, inc=1, device_id={"tok": lax.rem(me_tok + o, n_tok)}, device_id_type=MESH
            )
        greeted += n_tok - 1
    pl.semaphore_wait(barrier, greeted)

    def weight_copy(l, kind, o):
        if kind == 0:
            cols = up_in.shape[-1]
            src = up_in.at[l]
            dst = upg[l].at[:, :, :, pl.ds(pl.multiple_of(me_tok * cols, cols), cols)]
        else:
            cols = down_in.shape[-2]
            src = down_in.at[l]
            dst = downg[l].at[:, :, pl.ds(pl.multiple_of(me_tok * cols, cols), cols), :]
        if o == 0:
            return pltpu.make_async_copy(src, dst, wloc.at[l, kind])
        return pltpu.make_async_remote_copy(
            src_ref=src,
            dst_ref=dst,
            send_sem=wsend.at[l, kind, o - 1],
            recv_sem=wrecv.at[l, kind, o - 1],
            device_id={"tok": lax.rem(me_tok + o, n_tok)},
            device_id_type=MESH,
        )

    def start_weights():
        for l in range(layers):
            for kind in range(2):
                for o in range(n_tok):
                    weight_copy(l, kind, o).start()

    prepared = set()

    def prepare(l, kind):
        if (l, kind) in prepared:
            return
        prepared.add((l, kind))
        if gather:
            for o in range(n_tok):
                copy = weight_copy(l, kind, o)
                copy.wait() if o == 0 else copy.wait_recv()
        order = []
        for b in range(levels):
            at = 0
            for k in range(levels):
                at = jnp.maximum(at, jnp.where(level_bits[l, k] == b, 1 + k, 0))
            order.append(at)
        for j in range(blocks):
            if kind == 0:
                wup[l, j, pl.ds(0, wb), :] = upg[l][j, 0]
                for b in range(levels):
                    wup[l, j, pl.ds((1 + b) * wb, wb), :] = upg[l][j, order[b]]
                wup[l, j, pl.ds((1 + levels) * wb, rank), :] = rank_up[l, :, pl.ds(j * hb, hb)]
            else:
                wdown[l, j, pl.ds(0, wb), :] = downg[l][j, 0]
                for b in range(levels):
                    wdown[l, j, pl.ds((1 + b) * wb, wb), :] = downg[l][j, order[b]]

    def x_copy(l, c, b):
        at = pl.ds(c * cr, cr)
        return pltpu.make_async_remote_copy(
            src_ref=xbuf.at[l, at, :],
            dst_ref=xrecv.at[l, b, at, :],
            send_sem=xs_sem.at[l, c, b],
            recv_sem=xr_sem.at[l, c, b],
            device_id={"feat": partner[b]},
            device_id_type=MESH,
        )

    def t_copy(l, c, b):
        at = pl.ds(c * cr, cr)
        return pltpu.make_async_remote_copy(
            src_ref=tsend.at[l, b, at, :],
            dst_ref=trecv.at[l, b, at, :],
            send_sem=ts_sem.at[l, c, b],
            recv_sem=tr_sem.at[l, c, b],
            device_id={"feat": partner[b]},
            device_id_type=MESH,
        )

    last = nb - 1
    sizes = [cr >> (k + 1) for k in range(last)]
    own_at = [0]
    for k in range(last):
        own_at.append(own_at[-1] + mybit[k] * sizes[k])
    away_at = [own_at[k] + (1 - mybit[k]) * sizes[k] for k in range(last)]
    piece = cr >> last
    half_at = [sum(sizes[:k]) for k in range(last + 1)]
    half_rows = half_at[-1] + piece

    def reduce_copy(u, c, k):
        if k < last:
            src = part.at[u, pl.ds(pl.multiple_of(c * cr + away_at[k], sizes[k]), sizes[k]), :]
            size = sizes[k]
        else:
            src = part.at[u, pl.ds(pl.multiple_of(c * cr + own_at[last], piece), piece), :]
            size = piece
        return pltpu.make_async_remote_copy(
            src_ref=src,
            dst_ref=half.at[u, pl.ds(c * half_rows + half_at[k], size), :],
            send_sem=as_sem.at[u, c, k],
            recv_sem=ar_sem.at[u, c, k],
            device_id={"feat": partner[k]},
            device_id_type=MESH,
        )

    def spread_copy(u, c, k):
        size = cr >> (k + 1)
        at = pl.ds(pl.multiple_of(c * cr + own_at[k + 1], size), size)
        return pltpu.make_async_remote_copy(
            src_ref=full.at[u, at, :],
            dst_ref=full.at[u, at, :],
            send_sem=as_sem.at[u, c, nb + k],
            recv_sem=ar_sem.at[u, c, nb + k],
            device_id={"feat": partner[k]},
            device_id_type=MESH,
        )

    def start_bulk(u, c, stage):
        for b in reversed(range(nb)):
            if min(LATER, nb) * (0 if b == last else 1) == stage:
                (t_copy if u % 2 else x_copy)(u // 2, c, b).start()

    def sum_stage(u, c, k):
        reduce_copy(u, c, k).wait_recv()
        size = sizes[k] if k < last else piece
        start = own_at[k + 1] if k < last else own_at[last]
        at = pl.ds(pl.multiple_of(c * cr + start, size), size)
        total = part[u, at, :].astype(jnp.float32) + half[
            u, pl.ds(c * half_rows + half_at[k], size), :
        ].astype(jnp.float32)
        if k < last:
            part[u, at, :] = total.astype(jnp.bfloat16)
            reduce_copy(u, c, k + 1).start()
        else:
            full[u, at, :] = total.astype(jnp.bfloat16)
            if last > 0:
                spread_copy(u, c, last - 1).start()
        start_bulk(u, c, k + 1)

    def spread_stage(u, c, k):
        spread_copy(u, c, k).wait_recv()
        if k > 0:
            spread_copy(u, c, k - 1).start()

    def sum_stages(u, c):
        found = [functools.partial(sum_stage, u, c, k) for k in range(nb)]
        for k in range(last - 1, 0, -1):
            found.append(functools.partial(spread_stage, u, c, k))
        return found

    def finish_sum(u, c):
        if last > 0:
            spread_stage(u, c, 0)

    def begin(l, c):
        at = pl.ds(c * cr, cr)
        u = 2 * l
        x = xbuf[l, at, :]
        mine = rank_in[l, pl.ds(pl.multiple_of(me * width, width), width), :]
        part[u, at, :] = jnp.dot(x, mine, preferred_element_type=jnp.float32).astype(jnp.bfloat16)
        reduce_copy(u, c, 0).start()
        start_bulk(u, c, 0)

    def first(c):
        at = pl.ds(c * cr, cr)
        xbuf[0, at, :] = tokens[at, :]
        begin(0, c)

    def middle(l, c):
        at = pl.ds(c * cr, cr)
        u = 2 * l + 1
        prepare(l, 0)
        finish_sum(u - 1, c)
        for b in range(nb):
            x_copy(l, c, b).wait_recv()
        for j in range(blocks):
            pieces = [xbuf[l, at, pl.ds(j * wb, wb)]]
            for b in range(local_bits):
                pieces.append(xbuf[l, at, pl.ds((j ^ (1 << b)) * wb, wb)])
            for b in range(nb):
                pieces.append(xrecv[l, b, at, pl.ds(j * wb, wb)])
            pieces.append(full[u - 1, at, :])
            pre = jnp.dot(
                jnp.concatenate(pieces, axis=1), wup[l, j], preferred_element_type=jnp.float32
            )
            act = 0.5 * pre * (1.0 + lax.erf(pre * (1.0 / math.sqrt(2.0))))
            hid[at, pl.ds(j * hb, hb)] = act.astype(jnp.bfloat16)
        part[u, at, :] = jnp.dot(
            hid[at, :], rank_down[l], preferred_element_type=jnp.float32
        ).astype(jnp.bfloat16)
        reduce_copy(u, c, 0).start()
        prepare(l, 1)
        own = [None] * blocks
        for j in range(blocks):
            out_j = lax.dot_general(
                hid[at, pl.ds(j * hb, hb)],
                wdown[l, j],
                (((1,), (1,)), ((), ())),
                preferred_element_type=jnp.float32,
            )
            terms = [out_j[:, k * wb : (k + 1) * wb] for k in range(1 + levels)]
            for b in range(nb):
                tsend[l, b, at, pl.ds(j * wb, wb)] = terms[1 + local_bits + b].astype(jnp.bfloat16)
            for to, value in [(j, terms[0])] + [(j ^ (1 << b), terms[1 + b]) for b in range(local_bits)]:
                own[to] = value if own[to] is None else own[to] + value
        start_bulk(u, c, 0)
        for j in range(blocks):
            col = pl.ds(j * wb, wb)
            acc[at, col] = own[j] + xbuf[l, at, col].astype(jnp.float32)

    def close(l, c):
        at = pl.ds(c * cr, cr)
        u = 2 * l + 1
        finish_sum(u, c)
        total = acc[at, :] + jnp.dot(full[u, at, :], rank_out[l], preferred_element_type=jnp.float32)
        for b in range(nb):
            t_copy(l, c, b).wait_recv()
            total = total + trecv[l, b, at, :].astype(jnp.float32)
        result = total.astype(jnp.bfloat16)
        if l + 1 < layers:
            xbuf[l + 1, at, :] = result
            begin(l + 1, c)
        else:
            out[at, :] = result

    plan = []
    for c in range(chunks):
        steps = [functools.partial(first, c)]
        for l in range(layers):
            steps += sum_stages(2 * l, c)
            steps.append(functools.partial(middle, l, c))
            steps += sum_stages(2 * l + 1, c)
            steps.append(functools.partial(close, l, c))
        plan.append(steps)

    plan[0][0]()
    if gather:
        start_weights()
    for tick in range(1, len(plan[0]) + cfg["skew"] * (chunks - 1)):
        for c in range(chunks):
            at = tick - cfg["skew"] * c
            if 0 <= at < len(plan[c]):
                plan[c][at]()

    for l in range(layers):
        if gather:
            for kind in range(2):
                for o in range(1, n_tok):
                    weight_copy(l, kind, o).wait_send()
        for c in range(chunks):
            for b in range(nb):
                x_copy(l, c, b).wait_send()
                t_copy(l, c, b).wait_send()
            for u in (2 * l, 2 * l + 1):
                for k in range(nb):
                    reduce_copy(u, c, k).wait_send()
                for k in range(last):
                    spread_copy(u, c, k).wait_send()


def per_device(tokens, level_bits, up_blocks, down_blocks, rank_in, rank_up, rank_down, rank_out):
    rows, width = tokens.shape
    layers, blocks, parts, wb, up_cols = up_blocks.shape
    hb, down_cols = down_blocks.shape[3:]
    n_tok, n_feat = lax.axis_size("tok"), lax.axis_size("feat")
    rank = rank_in.shape[-1]
    hidden = blocks * hb
    nb = bits_of(n_feat)
    chunk = min(CHUNK_ROWS, rows)
    chunks = rows // chunk
    gather = n_tok > 1 and up_cols % 128 == 0 and down_cols % 16 == 0
    if not gather:
        up_blocks = lax.all_gather(up_blocks, "tok", axis=4, tiled=True)
        down_blocks = lax.all_gather(down_blocks, "tok", axis=4, tiled=True)
    down_blocks = jnp.swapaxes(down_blocks, 3, 4)
    cfg = dict(
        layers=layers, rows=rows, width=width, blocks=blocks, wb=wb, hb=hb, n_feat=n_feat,
        n_tok=n_tok, rank=rank, chunk=chunk, gather=gather, skew=SKEW,
    )
    bf16 = jnp.bfloat16
    uses = 2 * layers
    half_rows = chunk
    scratch = [
        pltpu.VMEM((layers, rows, width), bf16),
        pltpu.VMEM((layers, nb, rows, width), bf16),
        pltpu.VMEM((layers, nb, rows, width), bf16),
        pltpu.VMEM((layers, nb, rows, width), bf16),
        pltpu.VMEM((uses, rows, rank), bf16),
        pltpu.VMEM((uses, chunks * half_rows, rank), bf16),
        pltpu.VMEM((uses, rows, rank), bf16),
        pltpu.VMEM((rows, hidden), bf16),
        pltpu.VMEM((rows, width), jnp.float32),
        pltpu.VMEM((layers, blocks, parts * wb + rank, hb), bf16),
        pltpu.VMEM((layers, blocks, parts * wb, hb), bf16),
    ]
    dma = pltpu.SemaphoreType.DMA
    if gather:
        scratch += [pltpu.VMEM((blocks, parts, wb, hb), bf16)] * (2 * layers)
        scratch += [
            dma((layers, 2, n_tok - 1)),
            dma((layers, 2, n_tok - 1)),
            dma((layers, 2)),
        ]
    scratch += [dma((layers, chunks, nb))] * 4 + [dma((uses, chunks, 2 * nb - 1))] * 2
    vmem = pl.BlockSpec(memory_space=pltpu.VMEM)
    smem = pl.BlockSpec(memory_space=pltpu.SMEM)
    return pl.pallas_call(
        functools.partial(network, cfg),
        out_shape=jax.ShapeDtypeStruct((rows, width), bf16),
        in_specs=[vmem, smem] + [vmem] * 6,
        out_specs=vmem,
        scratch_shapes=scratch,
        compiler_params=pltpu.CompilerParams(
            collective_id=0, has_side_effects=True, vmem_limit_bytes=63 * 1024 * 1024
        ),
    )(tokens, level_bits, up_blocks, down_blocks, rank_in, rank_up, rank_down, rank_out)


def solution(mesh):
    return jax.shard_map(
        per_device,
        mesh=mesh,
        in_specs=(
            P("tok", "feat"),
            P(),
            P(None, "feat", None, None, "tok"),
            P(None, "feat", None, None, "tok"),
            P(),
            P(None, None, "feat"),
            P(None, "feat", None),
            P(None, None, "feat"),
        ),
        out_specs=P("tok", "feat"),
        check_vma=False,
    )
```
